32 devices in a mesh: mem: 8 (over z, x), feat: 4 (over y, core).
Axes of the slice: x: 2, y: 2, z: 4, core: 2. Of those that a mesh axis runs over, the one named last changes fastest.
Arguments:
- events: bfloat16 [2048, 32, 256], P('mem'), may hold values from -6 to 6
- w_in: bfloat16 [256, 1024], P(None, 'feat'), may hold values from -0.375 to 0.375
- w_out: bfloat16 [1024, 256], P('feat'), may hold values from -0.1875 to 0.1875
- probe_vectors: bfloat16 [2048, 256], P(('mem', 'feat')), may hold values from -8 to 8
- key_queue: bfloat16 [65536, 256], P('mem'), may hold values from -1 to 1
- target_position: int32 [2048], P(('mem', 'feat')), may hold values from 0 to 65535
- pointer: int32 [1], replicated, may hold values from 0 to 65535
Outputs:
- loss: float32 [2048], P(('mem', 'feat'))
- probe_derivative: float32 [2048, 256], P(('mem', 'feat'))
- new_memory: bfloat16 [65536, 256], P('mem')
The draws below stay inside these ranges and needn't reach their ends.
All inputs are finite; a program needn't handle non-finite values.
Results may differ from the reference program's by a relative error of at most 0.0017.
Values may be sent and summed in bfloat16 or wider, within the bound.
A program may use at most 64 MiB of HBM per device.

```python
import jax
import jax.numpy as jnp
from jax import lax

D = 256
HID = 1024
EVENTS = 32
SESS_DEV = 256
SLOT_DEV = 8192
QUERIES = 2048
SESSIONS = 2048
SLOTS = 65536
N_MEM = 8


def shared_directions(key):
    norm_factor = 1.0 / jnp.sqrt(jnp.float32(D))
    first = jax.random.truncated_normal(jax.random.fold_in(key, 7), -6.0, 6.0, (16, D), jnp.float32) * norm_factor
    second = jax.random.truncated_normal(jax.random.fold_in(key, 8), -6.0, 6.0, (16, D), jnp.float32) * norm_factor
    first = jnp.clip(first, -0.9, 0.9)
    second = jnp.clip(second, -0.9, 0.9)
    return (first, 0.99 * first + 0.1 * second)


def draw_key_queue(key, part):
    values_drawn = jax.random.truncated_normal(jax.random.fold_in(key, 1), -6.0, 6.0, (SLOTS, D), jnp.float32) / 16.0
    first, twins = shared_directions(key)
    planted_rows = jnp.arange(16, dtype=jnp.int32) * (SLOTS // 16) + 3
    values_drawn = values_drawn.at[planted_rows].set(first)
    values_drawn = values_drawn.at[planted_rows + SLOTS // 32 + 5].set(twins)
    return jnp.clip(values_drawn, -1.0, 1.0).astype(jnp.bfloat16)


def draw_probe_vectors(key, part):
    values_drawn = jax.random.truncated_normal(jax.random.fold_in(key, 2), -6.0, 6.0, (QUERIES, D), jnp.float32) * 0.25
    first, twins = shared_directions(key)
    planted_rows = jnp.arange(16, dtype=jnp.int32) * (QUERIES // 16)
    strength = 9.0 + 9.0 * jnp.arange(16, dtype=jnp.float32) / 15.0
    values_drawn = values_drawn.at[planted_rows].set(jnp.clip(strength[:, None] * first, -8.0, 8.0))
    return values_drawn.astype(jnp.bfloat16)


def touch_ends(drawn, stream_key, low, high):
    extent = drawn.shape
    index_at = [jax.random.randint(jax.random.fold_in(stream_key, axis), (), 0, extent[axis]) for axis in range(len(extent))]
    drawn = drawn.at[tuple(index_at)].set(low)
    longest = extent.index(max(extent))
    index_at[longest] = (index_at[longest] + 1) % extent[longest]
    return drawn.at[tuple(index_at)].set(high)


def levels(own_key, dims, split, low, top_value):
    gain, own = 1.0, jax.random.fold_in(own_key, 6)
    for axis_at, shards_of in split:
        steps = jnp.exp(jax.random.uniform(jax.random.fold_in(own, axis_at), (shards_of,), jnp.float32, low / len(split), top_value / len(split)))
        gain = gain * jnp.repeat(steps, dims[axis_at] // shards_of).reshape([-1 if axis == axis_at else 1 for axis in range(len(dims))])
    return gain


def gaussian(rng, dims, spread, limit, cuts=(), kind=jnp.bfloat16):
    drawn = jax.random.normal(rng, dims, jnp.float32) * spread
    if len(cuts) > 0:
        drawn = levels(rng, dims, cuts, -0.22, 0.18) * drawn
    return jnp.clip(drawn, min=-limit, max=limit).astype(kind)


def setup_inputs(seed: int = 0) -> dict:
    arg_keys = jax.random.split(jax.random.key(seed), 8)
    return {
        "events": gaussian(arg_keys[0], (SESSIONS, EVENTS, D), 1.0, 6.0, ((0, 8),)),
        "w_in": gaussian(arg_keys[1], (D, HID), D ** -0.5, 0.375, ((1, 4),)),
        "w_out": gaussian(arg_keys[2], (HID, D), HID ** -0.5, 0.1875, ((0, 4),)),
        "probe_vectors": draw_probe_vectors(jax.random.fold_in(arg_keys[7], 71), 0),
        "key_queue": draw_key_queue(jax.random.fold_in(arg_keys[7], 71), 0),
        "target_position": touch_ends(jax.random.randint(arg_keys[5], (QUERIES,), 0, SLOTS), jax.random.fold_in(arg_keys[5], 1), 0, SLOTS - 1).astype(jnp.int32),
        "pointer": jax.random.randint(arg_keys[6], (1,), 0, SLOTS).astype(jnp.int32),
    }


inverse_softness = 14.0
epsilon = 1e-06

def encode_block(session_block, w_in, w_out):
    flattened = session_block.reshape(session_block.shape[0] * EVENTS, D)
    activation = jax.nn.gelu(jnp.dot(flattened, w_in, preferred_element_type=jnp.float32))
    pooled = lax.optimization_barrier(jnp.mean(activation.reshape(session_block.shape[0], EVENTS, HID), axis=1)).astype(jnp.bfloat16)
    raw_key = jnp.dot(pooled, w_out, preferred_element_type=jnp.float32)
    scaled = raw_key * lax.rsqrt(lax.optimization_barrier(jnp.mean(raw_key * raw_key, axis=1, keepdims=True)) + epsilon) / 16.0
    return scaled.astype(jnp.bfloat16)

def reference(events, w_in, w_out, probe_vectors, key_queue, target_position, pointer):

    def encode_one(session_block):
        return encode_block(session_block, w_in, w_out)
    keys = lax.map(encode_one, events.reshape(N_MEM, SESS_DEV, EVENTS, D)).reshape(N_MEM * SESS_DEV, D)
    query_count = probe_vectors.shape[0]
    slot_blocks = key_queue.reshape(N_MEM, SLOT_DEV, D)
    block_starts = jnp.arange(N_MEM, dtype=jnp.int32) * SLOT_DEV
    positions = jnp.arange(SLOT_DEV, dtype=jnp.int32)

    def first_pass(carry, item):
        running_max, running_sum, positive_score = carry
        queue_position_span, first_slot = item
        similarity_table = jnp.dot(probe_vectors, queue_position_span.T, preferred_element_type=jnp.float32) * inverse_softness
        new_max = jnp.maximum(running_max, lax.optimization_barrier(jnp.max(similarity_table, axis=1)))
        running_sum = running_sum * jnp.exp(running_max - new_max) + lax.optimization_barrier(jnp.sum(jnp.exp(similarity_table - new_max[:, None]), axis=1))
        hit = positions[None, :] == (target_position - first_slot)[:, None]
        positive_score = positive_score + lax.optimization_barrier(jnp.sum(jnp.where(hit, similarity_table, 0.0), axis=1))
        return ((new_max, running_sum, positive_score), None)
    start_carry = (jnp.full((query_count,), -jnp.inf, jnp.float32), jnp.zeros((query_count,), jnp.float32), jnp.zeros((query_count,), jnp.float32))
    (top, total, positive_score), unused = lax.scan(first_pass, start_carry, (slot_blocks, block_starts))
    loss = top + jnp.log(total) - positive_score

    def second_pass(collected_denominator, queue_position_span):
        similarity_table = jnp.dot(probe_vectors, queue_position_span.T, preferred_element_type=jnp.float32) * inverse_softness
        weights = (jnp.exp(similarity_table - top[:, None]) / total[:, None]).astype(jnp.bfloat16)
        return (collected_denominator + jnp.dot(weights, queue_position_span, preferred_element_type=jnp.float32), None)
    collected_denominator, unused = lax.scan(second_pass, jnp.zeros((query_count, D), jnp.float32), slot_blocks)
    probe_derivative = inverse_softness * (collected_denominator - jnp.take(key_queue, target_position, axis=0).astype(jnp.float32))
    slot_count = N_MEM * SLOT_DEV
    slot_ids = jnp.arange(slot_count, dtype=jnp.int32)
    offsets = (slot_ids - pointer[0]) % slot_count
    picked = jnp.take(keys, jnp.minimum(offsets, keys.shape[0] - 1), axis=0)
    new_memory = jnp.where((offsets < keys.shape[0])[:, None], picked, key_queue)
    return (loss, probe_derivative, new_memory)
```

```python
import functools

import jax
import jax.numpy as jnp
from jax import lax
from jax.experimental import pallas as pl
from jax.experimental.pallas import tpu as pltpu
from jax.sharding import PartitionSpec as P

inverse_softness = 14.0
epsilon = 1e-06
log2e = 1.4426950408889634
MESH = pl.DeviceIdType.MESH
VMEM = pl.BlockSpec(memory_space=pltpu.VMEM)
HBM = pl.BlockSpec(memory_space=pltpu.HBM)
STEP_VMEM = 56 * 1024 * 1024
FILL_VMEM = 61000 * 1024


def flip(v, k):
    b = 1
    while b <= k:
        if k & b:
            v = v + b * (1 - 2 * lax.rem(lax.div(v, b), 2))
        b *= 2
    return v


def bits_of(n):
    out, b = [], 1
    while b < n:
        out.append(b)
        b *= 2
    return out[::-1]


def low_bit(s):
    return s & (-s)


def query_order(n):
    return list(range(n // 2, n)) + list(range(n // 2))


def step_kernel(
    n, nf, slot_block, q_chunk,
    ev_hbm, w_in_hbm, w_out_hbm, probe_hbm, queue_hbm, target_hbm,
    loss_ref, grad_ref, keys_ref,
    ev, w_in, w_out, queue, q_all, t_all, wide, partial, part_in, pos, m_s, l_s, acc,
    picked, h_in, stat_out, stat_in, gout, g_in, sims,
    ev_sem, in_sem, queue_sem, q_ss, q_rs, t_ss, t_rs, p_ss, p_rs, k_ss, k_rs,
    s_ss, s_rs, g_ss, g_rs, h_ss, h_rs,
):
    me = lax.axis_index("mem")
    mf = lax.axis_index("feat")
    slots, width = queue.shape
    own = q_all.shape[0] // n
    rows_q = n * own
    piece = ev.shape[1]
    n_blk = slots // slot_block
    part_rows = partial.shape[1]
    per_event = piece // part_rows
    order = query_order(n)
    place = {s: i for i, s in enumerate(order)}
    feats = list(range(nf - 1, -1, -1))
    f32, bf16 = jnp.float32, jnp.bfloat16

    def mem_peer(k):
        return (flip(me, k), mf)

    def feat_peer(k):
        return (me, flip(mf, k))

    def remote(src, dst, ss, rs, to):
        return pltpu.make_async_remote_copy(
            src_ref=src, dst_ref=dst, send_sem=ss, recv_sem=rs, device_id=to, device_id_type=MESH
        )

    barrier = pltpu.get_barrier_semaphore()
    for k in range(1, n):
        pl.semaphore_signal(barrier, inc=1, device_id=mem_peer(k), device_id_type=MESH)
    for k in range(1, nf):
        pl.semaphore_signal(barrier, inc=1, device_id=feat_peer(k), device_id_type=MESH)

    def rows_at(s):
        return pl.ds(place[s] * own, own)

    w_in_copy = pltpu.make_async_copy(w_in_hbm, w_in, in_sem.at[0])
    w_out_copy = pltpu.make_async_copy(w_out_hbm, w_out, in_sem.at[1])
    probe_copy = pltpu.make_async_copy(probe_hbm, q_all.at[rows_at(0)], in_sem.at[2])
    target_copy = pltpu.make_async_copy(target_hbm, t_all.at[0], in_sem.at[3])

    def ev_copy(i):
        at = pl.ds(pl.multiple_of(flip(mf, feats[i]) * piece, piece), piece)
        return pltpu.make_async_copy(ev_hbm.at[at], ev.at[i], ev_sem.at[i])

    def queue_copy(b):
        span = pl.ds(b * slot_block, slot_block)
        return pltpu.make_async_copy(queue_hbm.at[span], queue.at[span], queue_sem.at[b])

    w_in_copy.start()
    ev_copy(0).start()
    target_copy.start()
    w_out_copy.start()
    probe_copy.start()
    ahead = [ev_copy(i) for i in range(1, nf)] + [queue_copy(b) for b in range(n_blk)]

    def load_next(count):
        for a in ahead[:count]:
            a.start()
        del ahead[:count]

    load_next(1)

    pl.semaphore_wait(barrier, n - 1 + nf - 1)
    q_copies = {
        k: remote(probe_hbm, q_all.at[rows_at(k)], q_ss.at[k], q_rs.at[k], mem_peer(k))
        for k in range(n - 1, 0, -1)
    }
    t_copies = {
        k: remote(target_hbm, t_all.at[k], t_ss.at[k], t_rs.at[k], mem_peer(k))
        for k in range(n - 1, 0, -1)
    }
    for a in t_copies.values():
        a.start()
    for a in q_copies.values():
        a.start()

    c1 = 0.7978845608028654
    c2 = c1 * 0.044715

    def project(i):
        ev_copy(i).wait()
        load_next(len(ahead) if i == nf - 1 else 1)
        wide[i % 2] = jnp.dot(ev[i], w_in[...], preferred_element_type=f32)

    def encode(i):
        if i + 1 < nf:
            project(i + 1)
        x = wide[i % 2]
        y = x * jnp.tanh(x * (c1 + c2 * (x * x))) + x
        y = y.reshape(part_rows, per_event, y.shape[1])
        mean = jnp.sum(y, axis=1) * (0.5 / per_event)
        partial[feats[i]] = jnp.dot(mean.astype(bf16), w_out[...], preferred_element_type=f32)

    p_copies = []

    def send_partial(i):
        f = feats[i]
        if f:
            a = remote(partial.at[f], part_in.at[f], p_ss.at[f], p_rs.at[f], feat_peer(f))
            a.start()
            p_copies.append(a)

    w_in_copy.wait()
    project(0)
    w_out_copy.wait()
    for i in range(nf):
        encode(i)
        send_partial(i)
    probe_copy.wait()
    target_copy.wait()

    diag = lax.broadcasted_iota(jnp.int32, (own, own), 0) == lax.broadcasted_iota(
        jnp.int32, (own, own), 1
    )

    def as_column(row):
        wide_row = jnp.broadcast_to(row, (own, own))
        return jnp.sum(jnp.where(diag, wide_row, 0.0), axis=1, keepdims=True)

    chunk_blocks = q_chunk // own
    n_chunk = rows_q // q_chunk

    def slots_of(c):
        return order[c * chunk_blocks : (c + 1) * chunk_blocks]

    at = lax.broadcasted_iota(jnp.int32, (q_chunk, slot_block), 1)

    def pick(c):
        rs = slice(c * q_chunk, (c + 1) * q_chunk)
        for s in slots_of(c):
            if s:
                t_copies[s].wait_recv()
            local = as_column(t_all[s].astype(f32)).astype(jnp.int32) - me * slots
            pos[place[s] * own : (place[s] + 1) * own, :] = jnp.broadcast_to(local, (own, 128))
        for b in range(n_blk):
            if c == 0:
                queue_copy(b).wait()
            hit = at == (pos[rs, :1] - b * slot_block)
            v = jnp.dot(
                jnp.where(hit, 1.0, 0.0).astype(bf16),
                queue[b * slot_block : (b + 1) * slot_block, :],
                preferred_element_type=f32,
            )
            if b == 0:
                acc[rs, :] = v
            else:
                acc[rs, :] += v
        for s in slots_of(c):
            picked[s] = acc[rows_at(s), :].astype(bf16)

    h_copies = {}

    def h_send(bit):
        for s in range(n):
            if s and low_bit(s) == bit:
                h_copies[s] = remote(picked.at[s], h_in.at[s], h_ss.at[s], h_rs.at[s], mem_peer(bit))
                h_copies[s].start()

    def h_take(bit):
        for s in range(n):
            if s and low_bit(s) == bit:
                h_copies[s].wait_recv()
                picked[s ^ bit] = picked[s ^ bit] + h_in[s]

    for c in range(n_chunk):
        pick(c)
    h_send(1)

    k_copies = {}

    def key_span(r):
        m, f = flip(me, r[0]), flip(mf, r[1])
        return pl.ds(pl.multiple_of((m * nf + f) * part_rows, part_rows), part_rows)

    def onward(r):
        m, f = r
        out = []
        if r == (0, 0):
            out += [("m", k) for k in range(n - 2, 0, -2)]
        if f == 0 and m % 2 == 0:
            out.append(("m", 1))
        return out + [("f", b) for b in bits_of(nf) if not f or b < low_bit(f)]

    def pass_on(*r):
        if r != (0, 0):
            k_copies[r].wait_recv()
        span = key_span(r)
        for axis, b in onward(r):
            to = mem_peer(b) if axis == "m" else feat_peer(b)
            d = (r[0] ^ b, r[1]) if axis == "m" else (r[0], r[1] ^ b)
            j = d[0] * nf + d[1]
            k_copies[d] = remote(keys_ref.at[span], keys_ref.at[span], k_ss.at[j], k_rs.at[j], to)
            k_copies[d].start()

    def make_keys():
        for a in p_copies:
            a.wait_recv()
        raw = partial[0]
        for f in range(1, nf):
            raw = raw + part_in[f]
        scaled = raw * lax.rsqrt(jnp.mean(raw * raw, axis=1, keepdims=True) + epsilon) / 16.0
        keys_ref[key_span((0, 0)), :] = scaled.astype(bf16)
        pass_on(0, 0)

    make_keys()

    scale2 = inverse_softness * log2e
    work = [(c, b) for c in range(n_chunk) for b in range(n_blk)]
    q_seen = set()

    def similar(i):
        c, b = work[i]
        for s in slots_of(c):
            if s and s not in q_seen:
                q_seen.add(s)
                q_copies[s].wait_recv()
        sims[i % 2] = lax.dot_general(
            q_all[c * q_chunk : (c + 1) * q_chunk, :],
            queue[b * slot_block : (b + 1) * slot_block, :],
            (((1,), (1,)), ((), ())),
            preferred_element_type=f32,
        )

    def attend(i):
        c, b = work[i]
        rs = slice(c * q_chunk, (c + 1) * q_chunk)
        if i + 1 < len(work):
            similar(i + 1)
        s = sims[i % 2]
        m_new = jnp.broadcast_to(jnp.max(s, axis=1, keepdims=True), (q_chunk, 128))
        if b:
            m_old = m_s[rs, :]
            m_new = jnp.maximum(m_old, m_new)
            alpha = jnp.exp2((m_old - m_new) * scale2)
        m_s[rs, :] = m_new
        total, ps = None, []
        for j in range(slot_block // 128):
            p = jnp.exp2((s[:, j * 128 : (j + 1) * 128] - m_new) * scale2)
            total = p if total is None else total + p
            ps.append(p.astype(bf16))
        pv = jnp.dot(
            jnp.concatenate(ps, axis=1),
            queue[b * slot_block : (b + 1) * slot_block, :],
            preferred_element_type=f32,
        )
        if b:
            l_s[rs, :] = l_s[rs, :] * alpha + total
            for j in range(width // 128):
                cs = slice(j * 128, (j + 1) * 128)
                acc[rs, cs] = acc[rs, cs] * alpha + pv[:, cs]
        else:
            l_s[rs, :] = total
            acc[rs, :] = pv

    g_copies, s_copies = {}, {}

    def send_results(c):
        rs = slice(c * q_chunk, (c + 1) * q_chunk)
        for s in slots_of(c):
            if s:
                gout[s] = acc[rows_at(s), :].astype(bf16)
                g_copies[s] = remote(gout.at[s], g_in.at[s], g_ss.at[s], g_rs.at[s], mem_peer(s))
                g_copies[s].start()
        lane = lax.broadcasted_iota(jnp.int32, (q_chunk, 128), 1)
        sums = jnp.sum(l_s[rs, :], axis=1, keepdims=True)
        packed = jnp.where(lane == 0, m_s[rs, :], jnp.broadcast_to(sums, (q_chunk, 128))).T
        for i, s in enumerate(slots_of(c)):
            stat_out[s, 0:2, :] = packed[0:2, i * own : (i + 1) * own]
            if s:
                s_copies[s] = remote(stat_out.at[s], stat_in.at[s], s_ss.at[s], s_rs.at[s], mem_peer(s))
                s_copies[s].start()

    tasks = {}

    def later(frac, fn, *args):
        tasks.setdefault(int(frac * (len(work) - 1) + 0.5), []).append((fn, args))

    mem_bits = bits_of(n)[::-1]

    def step_h(j):
        h_take(mem_bits[j])
        if j + 1 < len(mem_bits):
            h_send(mem_bits[j + 1])

    for j in range(len(mem_bits) - 1):
        later((j + 1) / 2 if len(mem_bits) == 3 else (j + 1) / len(mem_bits), step_h, j)
    evens, odds = list(range(2, n, 2)), list(range(3, n, 2))
    for i, k in enumerate([1] + evens):
        later(3 / 7 + i / (7 * len(evens)), pass_on, k, 0)
    later(6 / 7, pass_on, 3, 0)

    similar(0)
    for i, (c, b) in enumerate(work):
        attend(i)
        if b == n_blk - 1:
            send_results(c)
        for fn, args in tasks.get(i, []):
            fn(*args)

    for k in odds[1:]:
        pass_on(k, 0)
    for b in bits_of(nf):
        for f in range(b, nf, b):
            if low_bit(f) == b and b > 1:
                for m in range(n):
                    pass_on(m, f)
    step_h(len(mem_bits) - 1)

    paired = picked[0].astype(f32)
    score = jnp.sum(q_all[rows_at(0), :].astype(f32) * paired, axis=1, keepdims=True)
    score = jnp.sum(
        jnp.where(diag, jnp.broadcast_to(score, (own, own)), 0.0), axis=0, keepdims=True
    )
    for k in range(1, n):
        s_copies[k].wait_recv()
    stats = [stat_out[0]] + [stat_in[k] for k in range(1, n)]
    top = stats[0][0:1, :]
    for st in stats[1:]:
        top = jnp.maximum(top, st[0:1, :])
    powers = [jnp.exp2((st[0:1, :] - top) * scale2) for st in stats]
    total = stats[0][1:2, :] * powers[0]
    for st, w in zip(stats[1:], powers[1:]):
        total = total + st[1:2, :] * w
    loss_ref[...] = (top - score) * inverse_softness + jnp.log(total)
    grad = acc[rows_at(0), :] * as_column(powers[0] / total)
    for k in [order[i] for i in range(n) if order[i]]:
        g_copies[k].wait_recv()
        grad = grad + g_in[k].astype(f32) * as_column(powers[k] / total)
    grad_ref[...] = inverse_softness * (grad - paired)

    for f in range(1, nf, 2):
        for m in range(n):
            pass_on(m, f)
    for group in (t_copies, q_copies, k_copies, h_copies, s_copies, g_copies):
        for a in group.values():
            a.wait_send()
    for a in p_copies:
        a.wait_send()


def fill_kernel(
    block, start_ref, keys_hbm, queue_ref, loss_in, grad_in,
    loss_ref, grad_ref, out_hbm,
    keys, rolled, merged, keys_sem, out_sem,
):
    start = start_ref[0]
    count = keys.shape[0]
    slots, width = queue_ref.shape
    phase = jnp.bitwise_and(start, 15)
    blocks = slots // block
    here = (start < slots) & (start + count > 0)
    keys_copy = pltpu.make_async_copy(keys_hbm, keys, keys_sem)

    @pl.when(here)
    def _():
        keys_copy.start()

    def spans(i):
        return slice(i * block, (i + 1) * block)

    def inside(i):
        return (i * block < start + count) & ((i + 1) * block > start)

    def plain(i):
        return pltpu.make_async_copy(queue_ref.at[spans(i)], out_hbm.at[spans(i)], out_sem.at[i])

    for i in range(blocks):

        @pl.when(jnp.logical_not(inside(i)))
        def _():
            plain(i).start()

    loss_ref[...] = loss_in[...]
    grad_ref[...] = grad_in[...]

    @pl.when(here)
    def _():
        keys_copy.wait()
        tile = min(256, count)
        for c in range(count // tile + 1):
            lo = max(c * tile - 16, 0)
            hi = min(c * tile + tile, count)
            x = keys[lo:hi, :].astype(jnp.float32)
            if c == 0:
                x = jnp.concatenate([jnp.zeros((16, width), jnp.float32), x], axis=0)
            if c == count // tile:
                x = jnp.concatenate([x, jnp.zeros((16, width), jnp.float32)], axis=0)
            x = pltpu.roll(x, phase, 0)[16:, :]
            at = block + c * tile
            rolled[at : at + x.shape[0], :] = x.astype(jnp.bfloat16)

    for i in range(blocks):

        @pl.when(inside(i))
        def _():
            at = pl.multiple_of(block + i * block - (start - phase), 16)
            row = lax.broadcasted_iota(jnp.int32, (block, width), 0) + (i * block - start)
            take = (row >= 0) & (row < count)
            new = rolled[pl.ds(at, block), :].astype(jnp.float32)
            old = queue_ref[spans(i), :].astype(jnp.float32)
            merged[spans(i), :] = jnp.where(take, new, old).astype(jnp.bfloat16)
            pltpu.make_async_copy(
                merged.at[spans(i)], out_hbm.at[spans(i)], out_sem.at[i]
            ).start()

    for i in range(blocks):
        plain(i).wait()


def shards(events, w_in, w_out, probe_vectors, key_queue, target_position, pointer):
    n, nf = lax.axis_size("mem"), lax.axis_size("feat")
    sessions, per, depth = events.shape
    own, width = probe_vectors.shape
    slots = key_queue.shape[0]
    rows_q = own * n
    hidden = w_in.shape[1]
    flat = events.reshape(sessions * per, depth)
    slot_block = min(2048, slots)
    q_chunk = min(256, rows_q)
    part_rows = sessions // nf
    piece = part_rows * per
    f32, bf16 = jnp.float32, jnp.bfloat16
    dma = pltpu.SemaphoreType.DMA
    loss, grad, keys = pl.pallas_call(
        functools.partial(step_kernel, n, nf, slot_block, q_chunk),
        out_shape=(
            jax.ShapeDtypeStruct((1, own), f32),
            jax.ShapeDtypeStruct((own, width), f32),
            jax.ShapeDtypeStruct((sessions * n, width), bf16),
        ),
        in_specs=[HBM] * 6,
        out_specs=(VMEM, VMEM, VMEM),
        scratch_shapes=[
            pltpu.VMEM((nf, piece, depth), bf16),
            pltpu.VMEM(w_in.shape, bf16),
            pltpu.VMEM(w_out.shape, bf16),
            pltpu.VMEM(key_queue.shape, bf16),
            pltpu.VMEM((rows_q, width), bf16),
            pltpu.VMEM((n, 1, own), jnp.int32),
            pltpu.VMEM((2, piece, hidden), f32),
            pltpu.VMEM((nf, part_rows, width), f32),
            pltpu.VMEM((nf, part_rows, width), f32),
            pltpu.VMEM((rows_q, 128), jnp.int32),
            pltpu.VMEM((rows_q, 128), f32),
            pltpu.VMEM((rows_q, 128), f32),
            pltpu.VMEM((rows_q, width), f32),
            pltpu.VMEM((n, own, width), bf16),
            pltpu.VMEM((n, own, width), bf16),
            pltpu.VMEM((n, 4, own), f32),
            pltpu.VMEM((n, 4, own), f32),
            pltpu.VMEM((n, own, width), bf16),
            pltpu.VMEM((n, own, width), bf16),
            pltpu.VMEM((2, q_chunk, slot_block), f32),
            dma((nf,)),
            dma((4,)),
            dma((slots // slot_block,)),
            dma((n,)), dma((n,)), dma((n,)), dma((n,)),
            dma((nf,)), dma((nf,)),
            dma((n * nf,)), dma((n * nf,)),
            dma((n,)), dma((n,)),
            dma((n,)), dma((n,)),
            dma((n,)), dma((n,)),
        ],
        compiler_params=pltpu.CompilerParams(
            collective_id=0, has_side_effects=True, vmem_limit_bytes=STEP_VMEM
        ),
        name="step",
    )(flat, w_in, w_out, probe_vectors, key_queue, target_position.reshape(1, own))

    slots_total = slots * n
    start = lax.rem(pointer - lax.axis_index("mem") * slots + slots_total, slots_total)
    count = sessions * n
    start = jnp.where(start > slots_total - count, start - slots_total, start)
    block = min(512, slots)
    loss, grad, new_memory = pl.pallas_call(
        functools.partial(fill_kernel, block),
        out_shape=(
            jax.ShapeDtypeStruct((1, own), f32),
            jax.ShapeDtypeStruct((own, width), f32),
            jax.ShapeDtypeStruct(key_queue.shape, bf16),
        ),
        in_specs=[pl.BlockSpec(memory_space=pltpu.SMEM), HBM, VMEM, VMEM, VMEM],
        out_specs=(VMEM, VMEM, HBM),
        scratch_shapes=[
            pltpu.VMEM((count, width), bf16),
            pltpu.VMEM((count + 2 * block + 16, width), bf16),
            pltpu.VMEM(key_queue.shape, bf16),
            dma,
            dma((slots // block,)),
        ],
        compiler_params=pltpu.CompilerParams(vmem_limit_bytes=FILL_VMEM),
        name="fill",
    )(start, keys, key_queue, loss, grad)
    return (loss.reshape(own), grad, new_memory)


def solution(mesh):
    placed = (
        P("mem", None, None),
        P(None, "feat"),
        P("feat", None),
        P(("mem", "feat"), None),
        P("mem", None),
        P(("mem", "feat")),
        P(),
    )
    return jax.shard_map(
        shards,
        mesh=mesh,
        in_specs=placed,
        out_specs=(P(("mem", "feat")), P(("mem", "feat"), None), P("mem", None)),
        check_vma=False,
    )
```

```python
import functools

import jax
import jax.numpy as jnp
from jax import lax
from jax.experimental import pallas as pl
from jax.experimental.pallas import tpu as pltpu
from jax.sharding import PartitionSpec as P

inverse_softness = 14.0
epsilon = 1e-06
log2e = 1.4426950408889634
MESH = pl.DeviceIdType.MESH
VMEM = pl.BlockSpec(memory_space=pltpu.VMEM)
HBM = pl.BlockSpec(memory_space=pltpu.HBM)
STEP_VMEM = 40 * 1024 * 1024
FILL_VMEM = 24 * 1024 * 1024


def flip(v, k):
    b = 1
    while b <= k:
        if k & b:
            v = v + b * (1 - 2 * lax.rem(lax.div(v, b), 2))
        b *= 2
    return v


def bits_of(n):
    out, b = [], 1
    while b < n:
        out.append(b)
        b *= 2
    return out[::-1]


def low_bit(s):
    return s & (-s)


def query_order(n):
    return list(range(n // 2, n)) + list(range(n // 2))


def step_kernel(
    n, nf, slot_block, q_chunk,
    ev_hbm, w_in_hbm, w_out_hbm, probe_hbm, queue_hbm, target_hbm,
    loss_ref, grad_ref, keys_ref,
    ev, w_in, w_out, queue, q_all, t_all, wide, partial, part_in, pos, m_s, l_s, acc,
    picked, h_in, stat_out, stat_in, gout, g_in, sims,
    ev_sem, in_sem, queue_sem, q_ss, q_rs, t_ss, t_rs, p_ss, p_rs, k_ss, k_rs,
    s_ss, s_rs, g_ss, g_rs, h_ss, h_rs,
):
    me = lax.axis_index("mem")
    mf = lax.axis_index("feat")
    slots, width = queue.shape
    own = q_all.shape[0] // n
    rows_q = n * own
    piece = ev.shape[1]
    n_blk = slots // slot_block
    part_rows = partial.shape[1]
    per_event = piece // part_rows
    order = query_order(n)
    place = {s: i for i, s in enumerate(order)}
    feats = list(range(nf - 1, -1, -1))
    f32, bf16 = jnp.float32, jnp.bfloat16

    def mem_peer(k):
        return (flip(me, k), mf)

    def feat_peer(k):
        return (me, flip(mf, k))

    def remote(src, dst, ss, rs, to):
        return pltpu.make_async_remote_copy(
            src_ref=src, dst_ref=dst, send_sem=ss, recv_sem=rs, device_id=to, device_id_type=MESH
        )

    barrier = pltpu.get_barrier_semaphore()
    for k in range(1, n):
        pl.semaphore_signal(barrier, inc=1, device_id=mem_peer(k), device_id_type=MESH)
    for k in range(1, nf):
        pl.semaphore_signal(barrier, inc=1, device_id=feat_peer(k), device_id_type=MESH)

    def rows_at(s):
        return pl.ds(place[s] * own, own)

    w_in_copy = pltpu.make_async_copy(w_in_hbm, w_in, in_sem.at[0])
    w_out_copy = pltpu.make_async_copy(w_out_hbm, w_out, in_sem.at[1])
    probe_copy = pltpu.make_async_copy(probe_hbm, q_all.at[rows_at(0)], in_sem.at[2])
    target_copy = pltpu.make_async_copy(target_hbm, t_all.at[0], in_sem.at[3])

    def ev_copy(i):
        at = pl.ds(pl.multiple_of(flip(mf, feats[i]) * piece, piece), piece)
        return pltpu.make_async_copy(ev_hbm.at[at], ev.at[i], ev_sem.at[i])

    def queue_copy(b):
        span = pl.ds(b * slot_block, slot_block)
        return pltpu.make_async_copy(queue_hbm.at[span], queue.at[span], queue_sem.at[b])

    w_in_copy.start()
    ev_copy(0).start()
    target_copy.start()
    w_out_copy.start()
    probe_copy.start()
    for i in range(1, nf):
        ev_copy(i).start()
    for b in range(n_blk):
        queue_copy(b).start()

    pl.semaphore_wait(barrier, n - 1 + nf - 1)
    q_copies = {
        k: remote(probe_hbm, q_all.at[rows_at(k)], q_ss.at[k], q_rs.at[k], mem_peer(k))
        for k in range(n - 1, 0, -1)
    }
    t_copies = {
        k: remote(target_hbm, t_all.at[k], t_ss.at[k], t_rs.at[k], mem_peer(k))
        for k in range(n - 1, 0, -1)
    }
    for a in t_copies.values():
        a.start()
    for a in q_copies.values():
        a.start()

    c1 = 0.7978845608028654
    c2 = c1 * 0.044715

    def project(i):
        wide[i % 2] = jnp.dot(ev[i], w_in[...], preferred_element_type=f32)

    def encode(i):
        if i + 1 < nf:
            project(i + 1)
        x = wide[i % 2]
        y = x * jnp.tanh(x * (c1 + c2 * (x * x))) + x
        y = y.reshape(part_rows, per_event, y.shape[1])
        mean = jnp.sum(y, axis=1) * (0.5 / per_event)
        partial[feats[i]] = jnp.dot(mean.astype(bf16), w_out[...], preferred_element_type=f32)

    p_copies = []

    def send_partial(i):
        f = feats[i]
        if f:
            a = remote(partial.at[f], part_in.at[f], p_ss.at[f], p_rs.at[f], feat_peer(f))
            a.start()
            p_copies.append(a)

    w_in_copy.wait()
    ev_copy(0).wait()
    project(0)
    w_out_copy.wait()
    probe_copy.wait()
    target_copy.wait()
    for i in range(1, nf):
        ev_copy(i).wait()
    half = nf // 2
    for i in range(half):
        encode(i)
    for i in range(half):
        send_partial(i)
    for i in range(half, nf):
        encode(i)
    for i in range(half, nf):
        send_partial(i)

    diag = lax.broadcasted_iota(jnp.int32, (own, own), 0) == lax.broadcasted_iota(
        jnp.int32, (own, own), 1
    )

    def as_column(row):
        wide_row = jnp.broadcast_to(row, (own, own))
        return jnp.sum(jnp.where(diag, wide_row, 0.0), axis=1, keepdims=True)

    chunk_blocks = q_chunk // own
    n_chunk = rows_q // q_chunk

    def slots_of(c):
        return order[c * chunk_blocks : (c + 1) * chunk_blocks]

    at = lax.broadcasted_iota(jnp.int32, (q_chunk, slot_block), 1)

    def pick(c):
        rs = slice(c * q_chunk, (c + 1) * q_chunk)
        for s in slots_of(c):
            local = as_column(t_all[s].astype(f32)).astype(jnp.int32) - me * slots
            pos[place[s] * own : (place[s] + 1) * own, :] = jnp.broadcast_to(local, (own, 128))
        for b in range(n_blk):
            hit = at == (pos[rs, :1] - b * slot_block)
            v = jnp.dot(
                jnp.where(hit, 1.0, 0.0).astype(bf16),
                queue[b * slot_block : (b + 1) * slot_block, :],
                preferred_element_type=f32,
            )
            if b == 0:
                acc[rs, :] = v
            else:
                acc[rs, :] += v
        for s in slots_of(c):
            picked[s] = acc[rows_at(s), :].astype(bf16)

    h_copies = {}

    def h_send(bit):
        for s in range(n):
            if s and low_bit(s) == bit:
                h_copies[s] = remote(picked.at[s], h_in.at[s], h_ss.at[s], h_rs.at[s], mem_peer(bit))
                h_copies[s].start()

    def h_take(bit):
        for s in range(n):
            if s and low_bit(s) == bit:
                h_copies[s].wait_recv()
                picked[s ^ bit] = picked[s ^ bit] + h_in[s]

    for k in range(1, n):
        t_copies[k].wait_recv()
    for b in range(n_blk):
        queue_copy(b).wait()
    for c in range(n_chunk):
        pick(c)
    h_send(1)

    k_copies = {}

    def key_span(r):
        m, f = flip(me, r[0]), flip(mf, r[1])
        return pl.ds(pl.multiple_of((m * nf + f) * part_rows, part_rows), part_rows)

    def onward(r):
        m, f = r
        out = []
        if r == (0, 0):
            out += [("m", k) for k in range(n - 2, 0, -2)]
        if f == 0 and m % 2 == 0:
            out.append(("m", 1))
        return out + [("f", b) for b in bits_of(nf) if not f or b < low_bit(f)]

    def pass_on(*r):
        if r != (0, 0):
            k_copies[r].wait_recv()
        span = key_span(r)
        for axis, b in onward(r):
            to = mem_peer(b) if axis == "m" else feat_peer(b)
            d = (r[0] ^ b, r[1]) if axis == "m" else (r[0], r[1] ^ b)
            j = d[0] * nf + d[1]
            k_copies[d] = remote(keys_ref.at[span], keys_ref.at[span], k_ss.at[j], k_rs.at[j], to)
            k_copies[d].start()

    def make_keys():
        for a in p_copies:
            a.wait_recv()
        raw = partial[0]
        for f in range(1, nf):
            raw = raw + part_in[f]
        scaled = raw * lax.rsqrt(jnp.mean(raw * raw, axis=1, keepdims=True) + epsilon) / 16.0
        keys_ref[key_span((0, 0)), :] = scaled.astype(bf16)
        pass_on(0, 0)

    make_keys()

    scale2 = inverse_softness * log2e
    work = [(c, b) for c in range(n_chunk) for b in range(n_blk)]
    q_seen = set()

    def similar(i):
        c, b = work[i]
        for s in slots_of(c):
            if s and s not in q_seen:
                q_seen.add(s)
                q_copies[s].wait_recv()
        sims[i % 2] = lax.dot_general(
            q_all[c * q_chunk : (c + 1) * q_chunk, :],
            queue[b * slot_block : (b + 1) * slot_block, :],
            (((1,), (1,)), ((), ())),
            preferred_element_type=f32,
        )

    def attend(i):
        c, b = work[i]
        rs = slice(c * q_chunk, (c + 1) * q_chunk)
        if i + 1 < len(work):
            similar(i + 1)
        s = sims[i % 2]
        m_new = jnp.broadcast_to(jnp.max(s, axis=1, keepdims=True), (q_chunk, 128))
        if b:
            m_old = m_s[rs, :]
            m_new = jnp.maximum(m_old, m_new)
            alpha = jnp.exp2((m_old - m_new) * scale2)
        m_s[rs, :] = m_new
        total, ps = None, []
        for j in range(slot_block // 128):
            p = jnp.exp2((s[:, j * 128 : (j + 1) * 128] - m_new) * scale2)
            total = p if total is None else total + p
            ps.append(p.astype(bf16))
        pv = jnp.dot(
            jnp.concatenate(ps, axis=1),
            queue[b * slot_block : (b + 1) * slot_block, :],
            preferred_element_type=f32,
        )
        if b:
            l_s[rs, :] = l_s[rs, :] * alpha + total
            for j in range(width // 128):
                cs = slice(j * 128, (j + 1) * 128)
                acc[rs, cs] = acc[rs, cs] * alpha + pv[:, cs]
        else:
            l_s[rs, :] = total
            acc[rs, :] = pv

    g_copies, s_copies = {}, {}

    def send_results(c):
        rs = slice(c * q_chunk, (c + 1) * q_chunk)
        for s in slots_of(c):
            if s:
                gout[s] = acc[rows_at(s), :].astype(bf16)
                g_copies[s] = remote(gout.at[s], g_in.at[s], g_ss.at[s], g_rs.at[s], mem_peer(s))
                g_copies[s].start()
        lane = lax.broadcasted_iota(jnp.int32, (q_chunk, 128), 1)
        sums = jnp.sum(l_s[rs, :], axis=1, keepdims=True)
        packed = jnp.where(lane == 0, m_s[rs, :], jnp.broadcast_to(sums, (q_chunk, 128))).T
        for i, s in enumerate(slots_of(c)):
            stat_out[s, 0:2, :] = packed[0:2, i * own : (i + 1) * own]
            if s:
                s_copies[s] = remote(stat_out.at[s], stat_in.at[s], s_ss.at[s], s_rs.at[s], mem_peer(s))
                s_copies[s].start()

    tasks = {}

    def later(frac, fn, *args):
        tasks.setdefault(int(frac * (len(work) - 1) + 0.5), []).append((fn, args))

    mem_bits = bits_of(n)[::-1]

    def step_h(j):
        h_take(mem_bits[j])
        if j + 1 < len(mem_bits):
            h_send(mem_bits[j + 1])

    evens, odds = list(range(2, n, 2)), list(range(3, n, 2))
    for k in [1, 2]:
        later(3 / 7, pass_on, k, 0)
    for k in evens[1:]:
        later(5 / 7, pass_on, k, 0)
    later(5 / 7, step_h, 0)
    later(1, pass_on, 3, 0)

    similar(0)
    for i, (c, b) in enumerate(work):
        attend(i)
        if b == n_blk - 1:
            send_results(c)
        for fn, args in tasks.get(i, []):
            fn(*args)

    for k in odds[1:]:
        pass_on(k, 0)
    step_h(1)
    for b in bits_of(nf):
        for f in range(b, nf, b):
            if low_bit(f) == b and b > 1:
                for m in range(n):
                    pass_on(m, f)
    for j in range(2, len(mem_bits)):
        step_h(j)

    paired = picked[0].astype(f32)
    score = jnp.sum(q_all[rows_at(0), :].astype(f32) * paired, axis=1, keepdims=True)
    score = jnp.sum(
        jnp.where(diag, jnp.broadcast_to(score, (own, own)), 0.0), axis=0, keepdims=True
    )
    for k in range(1, n):
        s_copies[k].wait_recv()
    stats = [stat_out[0]] + [stat_in[k] for k in range(1, n)]
    top = stats[0][0:1, :]
    for st in stats[1:]:
        top = jnp.maximum(top, st[0:1, :])
    powers = [jnp.exp2((st[0:1, :] - top) * scale2) for st in stats]
    total = stats[0][1:2, :] * powers[0]
    for st, w in zip(stats[1:], powers[1:]):
        total = total + st[1:2, :] * w
    loss_ref[...] = (top - score) * inverse_softness + jnp.log(total)
    grad = acc[rows_at(0), :] * as_column(powers[0] / total)
    for k in [order[i] for i in range(n) if order[i]]:
        g_copies[k].wait_recv()
        grad = grad + g_in[k].astype(f32) * as_column(powers[k] / total)
    grad_ref[...] = inverse_softness * (grad - paired)

    for f in range(1, nf, 2):
        for m in range(n):
            pass_on(m, f)
    for group in (t_copies, q_copies, k_copies, h_copies, s_copies, g_copies):
        for a in group.values():
            a.wait_send()
    for a in p_copies:
        a.wait_send()


def fill_kernel(
    block, start_ref, keys_hbm, queue_ref, loss_in, grad_in,
    loss_ref, grad_ref, out_hbm,
    keys, rolled, merged, keys_sem, out_sem,
):
    start = start_ref[0]
    count = keys.shape[0]
    slots, width = queue_ref.shape
    phase = jnp.bitwise_and(start, 15)
    blocks = slots // block
    here = (start < slots) & (start + count > 0)
    keys_copy = pltpu.make_async_copy(keys_hbm, keys, keys_sem)

    @pl.when(here)
    def _():
        keys_copy.start()

    def spans(i):
        return slice(i * block, (i + 1) * block)

    def inside(i):
        return (i * block < start + count) & ((i + 1) * block > start)

    def plain(i):
        return pltpu.make_async_copy(queue_ref.at[spans(i)], out_hbm.at[spans(i)], out_sem.at[i])

    for i in range(blocks):

        @pl.when(jnp.logical_not(inside(i)))
        def _():
            plain(i).start()

    loss_ref[...] = loss_in[...]
    grad_ref[...] = grad_in[...]

    @pl.when(here)
    def _():
        keys_copy.wait()
        tile = min(256, count)
        for c in range(count // tile + 1):
            lo = max(c * tile - 16, 0)
            hi = min(c * tile + tile, count)
            x = keys[lo:hi, :].astype(jnp.float32)
            if c == 0:
                x = jnp.concatenate([jnp.zeros((16, width), jnp.float32), x], axis=0)
            if c == count // tile:
                x = jnp.concatenate([x, jnp.zeros((16, width), jnp.float32)], axis=0)
            x = pltpu.roll(x, phase, 0)[16:, :]
            at = block + c * tile
            rolled[at : at + x.shape[0], :] = x.astype(jnp.bfloat16)

    for i in range(blocks):

        @pl.when(inside(i))
        def _():
            at = pl.multiple_of(block + i * block - (start - phase), 16)
            row = lax.broadcasted_iota(jnp.int32, (block, width), 0) + (i * block - start)
            take = (row >= 0) & (row < count)
            new = rolled[pl.ds(at, block), :].astype(jnp.float32)
            old = queue_ref[spans(i), :].astype(jnp.float32)
            merged[spans(i), :] = jnp.where(take, new, old).astype(jnp.bfloat16)
            pltpu.make_async_copy(
                merged.at[spans(i)], out_hbm.at[spans(i)], out_sem.at[i]
            ).start()

    for i in range(blocks):
        plain(i).wait()


def shards(events, w_in, w_out, probe_vectors, key_queue, target_position, pointer):
    n, nf = lax.axis_size("mem"), lax.axis_size("feat")
    sessions, per, depth = events.shape
    own, width = probe_vectors.shape
    slots = key_queue.shape[0]
    rows_q = own * n
    hidden = w_in.shape[1]
    flat = events.reshape(sessions * per, depth)
    slot_block = min(2048, slots)
    q_chunk = min(256, rows_q)
    part_rows = sessions // nf
    piece = part_rows * per
    f32, bf16 = jnp.float32, jnp.bfloat16
    dma = pltpu.SemaphoreType.DMA
    loss, grad, keys = pl.pallas_call(
        functools.partial(step_kernel, n, nf, slot_block, q_chunk),
        out_shape=(
            jax.ShapeDtypeStruct((1, own), f32),
            jax.ShapeDtypeStruct((own, width), f32),
            jax.ShapeDtypeStruct((sessions * n, width), bf16),
        ),
        in_specs=[HBM] * 6,
        out_specs=(VMEM, VMEM, VMEM),
        scratch_shapes=[
            pltpu.VMEM((nf, piece, depth), bf16),
            pltpu.VMEM(w_in.shape, bf16),
            pltpu.VMEM(w_out.shape, bf16),
            pltpu.VMEM(key_queue.shape, bf16),
            pltpu.VMEM((rows_q, width), bf16),
            pltpu.VMEM((n, 1, own), jnp.int32),
            pltpu.VMEM((2, piece, hidden), f32),
            pltpu.VMEM((nf, part_rows, width), f32),
            pltpu.VMEM((nf, part_rows, width), f32),
            pltpu.VMEM((rows_q, 128), jnp.int32),
            pltpu.VMEM((rows_q, 128), f32),
            pltpu.VMEM((rows_q, 128), f32),
            pltpu.VMEM((rows_q, width), f32),
            pltpu.VMEM((n, own, width), bf16),
            pltpu.VMEM((n, own, width), bf16),
            pltpu.VMEM((n, 4, own), f32),
            pltpu.VMEM((n, 4, own), f32),
            pltpu.VMEM((n, own, width), bf16),
            pltpu.VMEM((n, own, width), bf16),
            pltpu.VMEM((2, q_chunk, slot_block), f32),
            dma((nf,)),
            dma((4,)),
            dma((slots // slot_block,)),
            dma((n,)), dma((n,)), dma((n,)), dma((n,)),
            dma((nf,)), dma((nf,)),
            dma((n * nf,)), dma((n * nf,)),
            dma((n,)), dma((n,)),
            dma((n,)), dma((n,)),
            dma((n,)), dma((n,)),
        ],
        compiler_params=pltpu.CompilerParams(
            collective_id=0, has_side_effects=True, vmem_limit_bytes=STEP_VMEM
        ),
        name="step",
    )(
        *(
            pltpu.with_memory_space_constraint(a, pltpu.HBM)
            for a in (flat, w_in, w_out, probe_vectors, key_queue, target_position.reshape(1, own))
        )
    )

    slots_total = slots * n
    start = lax.rem(pointer - lax.axis_index("mem") * slots + slots_total, slots_total)
    count = sessions * n
    start = jnp.where(start > slots_total - count, start - slots_total, start)
    block = min(512, slots)
    loss, grad, new_memory = pl.pallas_call(
        functools.partial(fill_kernel, block),
        out_shape=(
            jax.ShapeDtypeStruct((1, own), f32),
            jax.ShapeDtypeStruct((own, width), f32),
            jax.ShapeDtypeStruct(key_queue.shape, bf16),
        ),
        in_specs=[pl.BlockSpec(memory_space=pltpu.SMEM), HBM, VMEM, VMEM, VMEM],
        out_specs=(VMEM, VMEM, HBM),
        scratch_shapes=[
            pltpu.VMEM((count, width), bf16),
            pltpu.VMEM((count + 2 * block + 16, width), bf16),
            pltpu.VMEM(key_queue.shape, bf16),
            dma,
            dma((slots // block,)),
        ],
        compiler_params=pltpu.CompilerParams(vmem_limit_bytes=FILL_VMEM),
        name="fill",
    )(start, keys, key_queue, loss, grad)
    return (loss.reshape(own), grad, new_memory)


def solution(mesh):
    placed = (
        P("mem", None, None),
        P(None, "feat"),
        P("feat", None),
        P(("mem", "feat"), None),
        P("mem", None),
        P(("mem", "feat")),
        P(),
    )
    return jax.shard_map(
        shards,
        mesh=mesh,
        in_specs=placed,
        out_specs=(P(("mem", "feat")), P(("mem", "feat"), None), P("mem", None)),
        check_vma=False,
    )
```

```python
import functools

import jax
import jax.numpy as jnp
from jax import lax
from jax.experimental import pallas as pl
from jax.experimental.pallas import tpu as pltpu
from jax.sharding import PartitionSpec as P

inverse_softness = 14.0
epsilon = 1e-06
log2e = 1.4426950408889634
MESH = pl.DeviceIdType.MESH
VMEM = pl.BlockSpec(memory_space=pltpu.VMEM)
HBM = pl.BlockSpec(memory_space=pltpu.HBM)
STEP_VMEM = 40 * 1024 * 1024
FILL_VMEM = 24 * 1024 * 1024


def flip(v, k):
    b = 1
    while b <= k:
        if k & b:
            v = v + b * (1 - 2 * lax.rem(lax.div(v, b), 2))
        b *= 2
    return v


def bits_of(n):
    out, b = [], 1
    while b < n:
        out.append(b)
        b *= 2
    return out[::-1]


def low_bit(s):
    return s & (-s)


def query_order(n):
    return list(range(n // 2, n)) + list(range(n // 2))


def step_kernel(
    n, nf, slot_block, q_chunk,
    ev_hbm, w_in_hbm, w_out_hbm, probe_hbm, queue_hbm, target_hbm,
    loss_ref, grad_ref, keys_ref, queue,
    ev, w_in, w_out, q_all, t_all, wide, partial, part_in, pos, m_s, l_s, acc,
    picked, h_in, stat_out, stat_in, gout, g_in, sims,
    ev_sem, in_sem, queue_sem, q_ss, q_rs, t_ss, t_rs, p_ss, p_rs, k_ss, k_rs,
    s_ss, s_rs, g_ss, g_rs, h_ss, h_rs,
):
    me = lax.axis_index("mem")
    mf = lax.axis_index("feat")
    slots, width = queue.shape
    own = q_all.shape[0] // n
    rows_q = n * own
    piece = ev.shape[1]
    n_blk = slots // slot_block
    part_rows = partial.shape[1]
    per_event = piece // part_rows
    order = query_order(n)
    place = {s: i for i, s in enumerate(order)}
    feats = list(range(nf - 1, -1, -1))
    f32, bf16 = jnp.float32, jnp.bfloat16

    def mem_peer(k):
        return (flip(me, k), mf)

    def feat_peer(k):
        return (me, flip(mf, k))

    def remote(src, dst, ss, rs, to):
        return pltpu.make_async_remote_copy(
            src_ref=src, dst_ref=dst, send_sem=ss, recv_sem=rs, device_id=to, device_id_type=MESH
        )

    barrier = pltpu.get_barrier_semaphore()
    for k in range(1, n):
        pl.semaphore_signal(barrier, inc=1, device_id=mem_peer(k), device_id_type=MESH)
    for k in range(1, nf):
        pl.semaphore_signal(barrier, inc=1, device_id=feat_peer(k), device_id_type=MESH)
    across = nf // 2
    diagonal = (flip(me, 1), flip(mf, across))
    pl.semaphore_signal(barrier, inc=1, device_id=diagonal, device_id_type=MESH)

    def rows_at(s):
        return pl.ds(place[s] * own, own)

    w_in_copy = pltpu.make_async_copy(w_in_hbm, w_in, in_sem.at[0])
    w_out_copy = pltpu.make_async_copy(w_out_hbm, w_out, in_sem.at[1])
    probe_copy = pltpu.make_async_copy(probe_hbm, q_all.at[rows_at(0)], in_sem.at[2])
    target_copy = pltpu.make_async_copy(target_hbm, t_all.at[0], in_sem.at[3])

    def ev_copy(i):
        at = pl.ds(pl.multiple_of(flip(mf, feats[i]) * piece, piece), piece)
        return pltpu.make_async_copy(ev_hbm.at[at], ev.at[i], ev_sem.at[i])

    def queue_copy(b):
        span = pl.ds(b * slot_block, slot_block)
        return pltpu.make_async_copy(queue_hbm.at[span], queue.at[span], queue_sem.at[b])

    w_in_copy.start()
    ev_copy(0).start()
    target_copy.start()
    w_out_copy.start()
    probe_copy.start()
    for i in range(1, nf):
        ev_copy(i).start()
    for b in range(n_blk):
        queue_copy(b).start()

    pl.semaphore_wait(barrier, n - 1 + nf - 1 + 1)
    q_copies = {
        k: remote(probe_hbm, q_all.at[rows_at(k)], q_ss.at[k], q_rs.at[k], mem_peer(k))
        for k in range(n - 1, 0, -1)
    }
    t_copies = {
        k: remote(target_hbm, t_all.at[k], t_ss.at[k], t_rs.at[k], mem_peer(k))
        for k in range(n - 1, 0, -1)
    }
    for a in t_copies.values():
        a.start()
    for a in q_copies.values():
        a.start()

    c1 = 0.7978845608028654
    c2 = c1 * 0.044715

    def project(i):
        wide[i % 2] = jnp.dot(ev[i], w_in[...], preferred_element_type=f32)

    def encode(i):
        if i + 1 < nf:
            project(i + 1)
        x = wide[i % 2]
        y = x * jnp.tanh(x * (c1 + c2 * (x * x))) + x
        y = y.reshape(part_rows, per_event, y.shape[1])
        mean = jnp.sum(y, axis=1) * (0.5 / per_event)
        partial[feats[i]] = jnp.dot(mean.astype(bf16), w_out[...], preferred_element_type=f32)

    p_copies = []

    def send_partial(i):
        f = feats[i]
        if f:
            a = remote(partial.at[f], part_in.at[f], p_ss.at[f], p_rs.at[f], feat_peer(f))
            a.start()
            p_copies.append(a)

    w_in_copy.wait()
    ev_copy(0).wait()
    project(0)
    w_out_copy.wait()
    probe_copy.wait()
    target_copy.wait()
    for i in range(1, nf):
        ev_copy(i).wait()
    half = nf // 2
    for i in range(half):
        encode(i)
    for i in range(half):
        send_partial(i)
    for i in range(half, nf):
        encode(i)
    for i in range(half, nf):
        send_partial(i)

    diag = lax.broadcasted_iota(jnp.int32, (own, own), 0) == lax.broadcasted_iota(
        jnp.int32, (own, own), 1
    )

    def as_column(row):
        wide_row = jnp.broadcast_to(row, (own, own))
        return jnp.sum(jnp.where(diag, wide_row, 0.0), axis=1, keepdims=True)

    chunk_blocks = q_chunk // own
    n_chunk = rows_q // q_chunk

    def slots_of(c):
        return order[c * chunk_blocks : (c + 1) * chunk_blocks]

    at = lax.broadcasted_iota(jnp.int32, (q_chunk, slot_block), 1)

    def pick(c):
        rs = slice(c * q_chunk, (c + 1) * q_chunk)
        for s in slots_of(c):
            local = as_column(t_all[s].astype(f32)).astype(jnp.int32) - me * slots
            pos[place[s] * own : (place[s] + 1) * own, :] = jnp.broadcast_to(local, (own, 128))
        for b in range(n_blk):
            hit = at == (pos[rs, :1] - b * slot_block)
            v = jnp.dot(
                jnp.where(hit, 1.0, 0.0).astype(bf16),
                queue[b * slot_block : (b + 1) * slot_block, :],
                preferred_element_type=f32,
            )
            if b == 0:
                acc[rs, :] = v
            else:
                acc[rs, :] += v
        for s in slots_of(c):
            picked[s] = acc[rows_at(s), :].astype(bf16)

    h_copies = {}

    def h_send(bit):
        for s in range(n):
            if s and low_bit(s) == bit:
                h_copies[s] = remote(picked.at[s], h_in.at[s], h_ss.at[s], h_rs.at[s], mem_peer(bit))
                h_copies[s].start()

    def h_take(bit):
        for s in range(n):
            if s and low_bit(s) == bit:
                h_copies[s].wait_recv()
                picked[s ^ bit] = picked[s ^ bit] + h_in[s]

    for k in range(1, n):
        t_copies[k].wait_recv()
    for b in range(n_blk):
        queue_copy(b).wait()
    for c in range(n_chunk):
        pick(c)
    h_send(1)

    k_copies = {}

    def key_span(r):
        m, f = flip(me, r[0]), flip(mf, r[1])
        return pl.ds(pl.multiple_of((m * nf + f) * part_rows, part_rows), part_rows)

    def onward(r):
        m, f = r
        out = []
        if r == (0, 0):
            out += [(k, 0) for k in range(n - 2, 0, -2)]
        if f == 0 and m % 2 == 0:
            out += [(1, 0), (0, across), (1, across)]
        return out + [(0, b) for b in bits_of(across) if not f or b < low_bit(f)]

    def pass_on(*r):
        if r != (0, 0):
            k_copies[r].wait_recv()
        span = key_span(r)
        for dm, df in onward(r):
            to = (flip(me, dm), flip(mf, df))
            d = (r[0] ^ dm, r[1] ^ df)
            j = d[0] * nf + d[1]
            k_copies[d] = remote(keys_ref.at[span], keys_ref.at[span], k_ss.at[j], k_rs.at[j], to)
            k_copies[d].start()

    def make_keys():
        for a in p_copies:
            a.wait_recv()
        raw = partial[0]
        for f in range(1, nf):
            raw = raw + part_in[f]
        scaled = raw * lax.rsqrt(jnp.mean(raw * raw, axis=1, keepdims=True) + epsilon) / 16.0
        keys_ref[key_span((0, 0)), :] = scaled.astype(bf16)
        pass_on(0, 0)

    make_keys()

    scale2 = inverse_softness * log2e
    work = [(c, b) for c in range(n_chunk) for b in range(n_blk)]
    q_seen = set()

    def similar(i):
        c, b = work[i]
        for s in slots_of(c):
            if s and s not in q_seen:
                q_seen.add(s)
                q_copies[s].wait_recv()
        sims[i % 2] = lax.dot_general(
            q_all[c * q_chunk : (c + 1) * q_chunk, :],
            queue[b * slot_block : (b + 1) * slot_block, :],
            (((1,), (1,)), ((), ())),
            preferred_element_type=f32,
        )

    def attend(i):
        c, b = work[i]
        rs = slice(c * q_chunk, (c + 1) * q_chunk)
        if i + 1 < len(work):
            similar(i + 1)
        s = sims[i % 2]
        m_new = jnp.broadcast_to(jnp.max(s, axis=1, keepdims=True), (q_chunk, 128))
        if b:
            m_old = m_s[rs, :]
            m_new = jnp.maximum(m_old, m_new)
            alpha = jnp.exp2((m_old - m_new) * scale2)
        m_s[rs, :] = m_new
        total, ps = None, []
        for j in range(slot_block // 128):
            p = jnp.exp2((s[:, j * 128 : (j + 1) * 128] - m_new) * scale2)
            total = p if total is None else total + p
            ps.append(p.astype(bf16))
        pv = jnp.dot(
            jnp.concatenate(ps, axis=1),
            queue[b * slot_block : (b + 1) * slot_block, :],
            preferred_element_type=f32,
        )
        if b:
            l_s[rs, :] = l_s[rs, :] * alpha + total
            for j in range(width // 128):
                cs = slice(j * 128, (j + 1) * 128)
                acc[rs, cs] = acc[rs, cs] * alpha + pv[:, cs]
        else:
            l_s[rs, :] = total
            acc[rs, :] = pv

    g_copies, s_copies = {}, {}

    def send_results(c):
        rs = slice(c * q_chunk, (c + 1) * q_chunk)
        for s in slots_of(c):
            if s:
                gout[s] = acc[rows_at(s), :].astype(bf16)
                g_copies[s] = remote(gout.at[s], g_in.at[s], g_ss.at[s], g_rs.at[s], mem_peer(s))
                g_copies[s].start()
        lane = lax.broadcasted_iota(jnp.int32, (q_chunk, 128), 1)
        sums = jnp.sum(l_s[rs, :], axis=1, keepdims=True)
        packed = jnp.where(lane == 0, m_s[rs, :], jnp.broadcast_to(sums, (q_chunk, 128))).T
        for i, s in enumerate(slots_of(c)):
            stat_out[s, 0:2, :] = packed[0:2, i * own : (i + 1) * own]
            if s:
                s_copies[s] = remote(stat_out.at[s], stat_in.at[s], s_ss.at[s], s_rs.at[s], mem_peer(s))
                s_copies[s].start()

    tasks = {}

    def later(frac, fn, *args):
        tasks.setdefault(int(frac * (len(work) - 1) + 0.5), []).append((fn, args))

    mem_bits = bits_of(n)[::-1]

    def step_h(j):
        h_take(mem_bits[j])
        if j + 1 < len(mem_bits):
            h_send(mem_bits[j + 1])

    evens, odds = list(range(2, n, 2)), list(range(3, n, 2))
    later(3 / 7, pass_on, 2, 0)
    for k in evens[1:]:
        later(5 / 7, pass_on, k, 0)
    later(5 / 7, step_h, 0)

    similar(0)
    for i, (c, b) in enumerate(work):
        attend(i)
        if b == n_blk - 1:
            send_results(c)
        for fn, args in tasks.get(i, []):
            fn(*args)

    step_h(1)
    pass_on(1, 0)
    for m in range(0, n, 2):
        pass_on(m, across)
    for m in range(3, n, 2):
        pass_on(m, 0)
    for m in range(1, n, 2):
        pass_on(m, across)
    for f in range(1, nf):
        if f != across and low_bit(f) > 1:
            for m in range(n):
                pass_on(m, f)
    for j in range(2, len(mem_bits)):
        step_h(j)

    paired = picked[0].astype(f32)
    score = jnp.sum(q_all[rows_at(0), :].astype(f32) * paired, axis=1, keepdims=True)
    score = jnp.sum(
        jnp.where(diag, jnp.broadcast_to(score, (own, own)), 0.0), axis=0, keepdims=True
    )
    for k in range(1, n):
        s_copies[k].wait_recv()
    stats = [stat_out[0]] + [stat_in[k] for k in range(1, n)]
    top = stats[0][0:1, :]
    for st in stats[1:]:
        top = jnp.maximum(top, st[0:1, :])
    powers = [jnp.exp2((st[0:1, :] - top) * scale2) for st in stats]
    total = stats[0][1:2, :] * powers[0]
    for st, w in zip(stats[1:], powers[1:]):
        total = total + st[1:2, :] * w
    loss_ref[...] = (top - score) * inverse_softness + jnp.log(total)
    grad = acc[rows_at(0), :] * as_column(powers[0] / total)
    for k in [order[i] for i in range(n) if order[i]]:
        g_copies[k].wait_recv()
        grad = grad + g_in[k].astype(f32) * as_column(powers[k] / total)
    grad_ref[...] = inverse_softness * (grad - paired)

    for f in range(1, nf, 2):
        for m in range(n):
            pass_on(m, f)
    for group in (t_copies, q_copies, k_copies, h_copies, s_copies, g_copies):
        for a in group.values():
            a.wait_send()
    for a in p_copies:
        a.wait_send()


def fill_kernel(
    block, start_ref, keys_hbm, queue_ref, loss_in, grad_in,
    loss_ref, grad_ref, out_hbm,
    keys, rolled, merged, keys_sem, out_sem,
):
    start = start_ref[0]
    count = keys.shape[0]
    slots, width = queue_ref.shape
    phase = jnp.bitwise_and(start, 15)
    blocks = slots // block
    here = (start < slots) & (start + count > 0)
    keys_copy = pltpu.make_async_copy(keys_hbm, keys, keys_sem)

    @pl.when(here)
    def _():
        keys_copy.start()

    def spans(i):
        return slice(i * block, (i + 1) * block)

    def inside(i):
        return (i * block < start + count) & ((i + 1) * block > start)

    def plain(i):
        return pltpu.make_async_copy(queue_ref.at[spans(i)], out_hbm.at[spans(i)], out_sem.at[i])

    for i in range(blocks):

        @pl.when(jnp.logical_not(inside(i)))
        def _():
            plain(i).start()

    loss_ref[...] = loss_in[...]
    grad_ref[...] = grad_in[...]

    @pl.when(here)
    def _():
        keys_copy.wait()
        tile = min(256, count)
        for c in range(count // tile + 1):
            lo = max(c * tile - 16, 0)
            hi = min(c * tile + tile, count)
            x = keys[lo:hi, :].astype(jnp.float32)
            if c == 0:
                x = jnp.concatenate([jnp.zeros((16, width), jnp.float32), x], axis=0)
            if c == count // tile:
                x = jnp.concatenate([x, jnp.zeros((16, width), jnp.float32)], axis=0)
            x = pltpu.roll(x, phase, 0)[16:, :]
            at = block + c * tile
            rolled[at : at + x.shape[0], :] = x.astype(jnp.bfloat16)

    for i in range(blocks):

        @pl.when(inside(i))
        def _():
            at = pl.multiple_of(block + i * block - (start - phase), 16)
            row = lax.broadcasted_iota(jnp.int32, (block, width), 0) + (i * block - start)
            take = (row >= 0) & (row < count)
            new = rolled[pl.ds(at, block), :].astype(jnp.float32)
            old = queue_ref[spans(i), :].astype(jnp.float32)
            merged[spans(i), :] = jnp.where(take, new, old).astype(jnp.bfloat16)
            pltpu.make_async_copy(
                merged.at[spans(i)], out_hbm.at[spans(i)], out_sem.at[i]
            ).start()

    for i in range(blocks):
        plain(i).wait()


def shards(events, w_in, w_out, probe_vectors, key_queue, target_position, pointer):
    n, nf = lax.axis_size("mem"), lax.axis_size("feat")
    sessions, per, depth = events.shape
    own, width = probe_vectors.shape
    slots = key_queue.shape[0]
    rows_q = own * n
    hidden = w_in.shape[1]
    flat = events.reshape(sessions * per, depth)
    slot_block = min(2048, slots)
    q_chunk = min(256, rows_q)
    part_rows = sessions // nf
    piece = part_rows * per
    f32, bf16 = jnp.float32, jnp.bfloat16
    dma = pltpu.SemaphoreType.DMA
    loss, grad, keys, held = pl.pallas_call(
        functools.partial(step_kernel, n, nf, slot_block, q_chunk),
        out_shape=(
            jax.ShapeDtypeStruct((1, own), f32),
            jax.ShapeDtypeStruct((own, width), f32),
            jax.ShapeDtypeStruct((sessions * n, width), bf16),
            jax.ShapeDtypeStruct(key_queue.shape, bf16),
        ),
        in_specs=[HBM] * 6,
        out_specs=(VMEM, VMEM, VMEM, VMEM),
        scratch_shapes=[
            pltpu.VMEM((nf, piece, depth), bf16),
            pltpu.VMEM(w_in.shape, bf16),
            pltpu.VMEM(w_out.shape, bf16),
            pltpu.VMEM((rows_q, width), bf16),
            pltpu.VMEM((n, 1, own), jnp.int32),
            pltpu.VMEM((2, piece, hidden), f32),
            pltpu.VMEM((nf, part_rows, width), f32),
            pltpu.VMEM((nf, part_rows, width), f32),
            pltpu.VMEM((rows_q, 128), jnp.int32),
            pltpu.VMEM((rows_q, 128), f32),
            pltpu.VMEM((rows_q, 128), f32),
            pltpu.VMEM((rows_q, width), f32),
            pltpu.VMEM((n, own, width), bf16),
            pltpu.VMEM((n, own, width), bf16),
            pltpu.VMEM((n, 4, own), f32),
            pltpu.VMEM((n, 4, own), f32),
            pltpu.VMEM((n, own, width), bf16),
            pltpu.VMEM((n, own, width), bf16),
            pltpu.VMEM((2, q_chunk, slot_block), f32),
            dma((nf,)),
            dma((4,)),
            dma((slots // slot_block,)),
            dma((n,)), dma((n,)), dma((n,)), dma((n,)),
            dma((nf,)), dma((nf,)),
            dma((n * nf,)), dma((n * nf,)),
            dma((n,)), dma((n,)),
            dma((n,)), dma((n,)),
            dma((n,)), dma((n,)),
        ],
        compiler_params=pltpu.CompilerParams(
            collective_id=0, has_side_effects=True, vmem_limit_bytes=STEP_VMEM
        ),
        name="step",
    )(
        *(
            pltpu.with_memory_space_constraint(a, pltpu.HBM)
            for a in (flat, w_in, w_out, probe_vectors, key_queue, target_position.reshape(1, own))
        )
    )

    slots_total = slots * n
    start = lax.rem(pointer - lax.axis_index("mem") * slots + slots_total, slots_total)
    count = sessions * n
    start = jnp.where(start > slots_total - count, start - slots_total, start)
    block = min(512, slots)
    loss, grad, new_memory = pl.pallas_call(
        functools.partial(fill_kernel, block),
        out_shape=(
            jax.ShapeDtypeStruct((1, own), f32),
            jax.ShapeDtypeStruct((own, width), f32),
            jax.ShapeDtypeStruct(key_queue.shape, bf16),
        ),
        in_specs=[pl.BlockSpec(memory_space=pltpu.SMEM), HBM, VMEM, VMEM, VMEM],
        out_specs=(VMEM, VMEM, HBM),
        scratch_shapes=[
            pltpu.VMEM((count, width), bf16),
            pltpu.VMEM((count + 2 * block + 16, width), bf16),
            pltpu.VMEM(key_queue.shape, bf16),
            dma,
            dma((slots // block,)),
        ],
        compiler_params=pltpu.CompilerParams(vmem_limit_bytes=FILL_VMEM),
        name="fill",
    )(start, keys, held, loss, grad)
    return (loss.reshape(own), grad, new_memory)


def solution(mesh):
    placed = (
        P("mem", None, None),
        P(None, "feat"),
        P("feat", None),
        P(("mem", "feat"), None),
        P("mem", None),
        P(("mem", "feat")),
        P(),
    )
    return jax.shard_map(
        shards,
        mesh=mesh,
        in_specs=placed,
        out_specs=(P(("mem", "feat")), P(("mem", "feat"), None), P("mem", None)),
        check_vma=False,
    )
```
